768 devices in a mesh: rows: 64 (over z_hi, y, core), cols: 12 (over x, z_lo).
Axes of the slice: x: 4, y: 8, z: 12 (z_hi: 4, z_lo: 3; z = z_hi * 3 + z_lo), core: 2. Of those that a mesh axis runs over, the one named last changes fastest.
Arguments:
- values: bfloat16 [49152, 6144], P('rows', 'cols'), may hold values from -6 to 6
- tile_scale: float32 [192, 24], P('rows', 'cols'), may hold values from 0.1 to 10
- occupancy: int32 [192, 24], P('rows', 'cols'), may hold values from 0 to 1, as said below
- row_kind: int32 [49152], P('rows'), may hold values 0 or 1
- right_side: float32 [128, 49152], P(None, 'rows'), may hold values from -6 to 6
- cost_vector: float32 [128, 6144], P(None, 'cols'), may hold values from -6 to 6
- lower_bound: float32 [6144], P('cols'), may hold values from -2 to -0.2
- upper_bound: float32 [6144], P('cols'), may hold values from 0.2 to 2
- x_start: float32 [128, 6144], P(None, 'cols'), may hold values from -3 to 3
- y_start: float32 [128, 49152], P(None, 'rows'), may hold values from -3 to 3
- step_sizes: float32 [2], replicated, may hold values from 0.005 to 0.02
Outputs:
- x_next: float32 [128, 6144], P(None, 'cols')
- y_next: float32 [128, 49152], P(None, 'rows')
- measures: float32 [3, 128], replicated
- primal_move: float32 [128], replicated
The draws below stay inside these ranges and needn't reach their ends.
Inputs may be any that keep to these rules, and one draw needn't show every extreme that they name: `occupancy`: every tile row and every tile column of 256 x 256 tiles holds at least one occupied tile.
All inputs are finite; a program needn't handle non-finite values. No bound on the sum of `row_kind` on one device may be relied on, other than what follows from the above.
Results may differ from the reference program's by a relative error of at most 0.00038.
Values sent between devices are 32-bit elements; how exact they have to be, the bound alone decides.
A program may use at most 32 MiB of HBM per device.

```python
import math
import jax
import jax.numpy as jnp
from jax import lax

TILE_WIDTH = 256
SCENARIOS = 128
ROWS_ALL = 49152
COLS_ALL = 6144


def draw_occupancy(key, part):
    tile_rows = ROWS_ALL // TILE_WIDTH
    tile_cols = COLS_ALL // TILE_WIDTH
    first_key = jax.random.fold_in(key, 11)
    second_key = jax.random.fold_in(key, 23)
    coin_flip = jax.random.randint(first_key, (tile_rows, tile_cols), 0, 2)
    offset = jax.random.randint(second_key, (), 0, tile_cols)
    band_mask = jnp.arange(tile_cols)[None, :] == (jnp.arange(tile_rows)[:, None] + offset) % tile_cols
    return jnp.maximum(coin_flip, band_mask.astype(jnp.int32)).astype(jnp.int32)


def place_ends(values, key, least, top_value):
    place = [jax.random.randint(jax.random.fold_in(key, axis), (), 0, length) for axis, length in enumerate(values.shape)]
    main_axis = values.shape.index(max(values.shape))
    beside = place[:main_axis] + [(place[main_axis] + 1) % values.shape[main_axis]] + place[main_axis + 1:]
    return values.at[tuple(place)].set(least).at[tuple(beside)].set(top_value)


def steps_of(key, dims, cuts, low, top_value):
    gain = 1.0
    for axis_at, parts in cuts:
        draws = jax.random.uniform(jax.random.fold_in(jax.random.fold_in(key, 6), axis_at), (parts,), jnp.float32, low / len(cuts), top_value / len(cuts))
        gain = gain * jnp.repeat(jnp.exp(draws), dims[axis_at] // parts).reshape((-1,) + (1,) * (len(dims) - 1 - axis_at))
    return gain


def noise(rng, extent, deviation, most, cuts=(), kind=jnp.bfloat16):
    factor_of = steps_of(rng, extent, cuts, -0.22, 0.18) if cuts else 1.0
    array = jax.random.normal(rng, extent, jnp.float32) * deviation * factor_of
    return jnp.minimum(jnp.maximum(array, -most), most).astype(kind)


def setup_inputs(seed: int = 0) -> dict:
    arg_keys = jax.random.split(jax.random.key(seed), 12)
    values = noise(arg_keys[0], (ROWS_ALL, COLS_ALL), 1.0, 6.0, ((0, 64), (1, 12)))
    tile_scale = jnp.clip(jnp.exp(math.log(10.0) - 4.6051702 * jax.random.uniform(arg_keys[1], (ROWS_ALL // TILE_WIDTH, COLS_ALL // TILE_WIDTH), jnp.float32) ** steps_of(arg_keys[1], (ROWS_ALL // TILE_WIDTH, COLS_ALL // TILE_WIDTH), ((0, 64), (1, 12)), -0.2, 0.2)), 0.1, 10.0)
    occupancy = draw_occupancy(jax.random.fold_in(arg_keys[11], 71), 0)
    row_kind = place_ends((jax.random.randint(arg_keys[3], (ROWS_ALL,), 0, 2) < 1).astype(jnp.int32), jax.random.fold_in(arg_keys[3], 1), 0, 1)
    right_side = noise(arg_keys[4], (SCENARIOS, ROWS_ALL), 1.0, 6.0, ((1, 64),), jnp.float32)
    cost_vector = noise(arg_keys[5], (SCENARIOS, COLS_ALL), 1.0, 6.0, ((1, 12),), jnp.float32)
    lower_bound = jnp.clip(-2.0 + 1.8 * jax.random.uniform(arg_keys[6], (COLS_ALL,), jnp.float32) ** steps_of(arg_keys[6], (COLS_ALL,), ((0, 12),), -0.2, 0.2), -2.0, -0.2)
    upper_bound = jnp.clip(0.2 + 1.8 * jax.random.uniform(arg_keys[7], (COLS_ALL,), jnp.float32) ** steps_of(arg_keys[7], (COLS_ALL,), ((0, 12),), -0.2, 0.2), 0.2, 2.0)
    x_start = noise(arg_keys[8], (SCENARIOS, COLS_ALL), 0.5, 3.0, ((1, 12),), jnp.float32)
    y_start = noise(arg_keys[9], (SCENARIOS, ROWS_ALL), 0.5, 3.0, ((1, 64),), jnp.float32)
    step_sizes = jnp.clip(jax.random.uniform(arg_keys[10], (2,), jnp.float32, 0.005, 0.02), 0.005, 0.02)
    return dict(values=values, tile_scale=tile_scale, occupancy=occupancy, row_kind=row_kind, right_side=right_side, cost_vector=cost_vector, lower_bound=lower_bound, upper_bound=upper_bound, x_start=x_start, y_start=y_start, step_sizes=step_sizes)


EPS = 1e-06

def reference(values, tile_scale, occupancy, row_kind, right_side, cost_vector, lower_bound, upper_bound, x_start, y_start, step_sizes):
    tile_rows = ROWS_ALL // TILE_WIDTH
    tile_cols = COLS_ALL // TILE_WIDTH
    factor = tile_scale * occupancy.astype(jnp.float32)
    blocks = values.reshape(tile_rows, TILE_WIDTH, tile_cols, TILE_WIDTH)

    def sweep_scales(row_scale, col_scale):
        col_tiles = col_scale.reshape(tile_cols, TILE_WIDTH)
        row_tiles = row_scale.reshape(tile_rows, TILE_WIDTH)

        def advance(running, scanned):
            block, weights, row_piece = scanned
            magnitude = jnp.abs(block).astype(jnp.float32) * weights[None, :, None]
            row_peak = lax.optimization_barrier(jnp.max(magnitude * col_tiles[None], axis=(1, 2)))
            col_peak = lax.optimization_barrier(jnp.max(magnitude * row_piece[:, None, None], axis=0))
            return (jnp.maximum(running, col_peak), row_peak)
        col_peak, row_peak = lax.scan(advance, jnp.zeros((tile_cols, TILE_WIDTH), jnp.float32), (blocks, factor, row_tiles))
        row_peak = row_peak.reshape(ROWS_ALL)
        col_peak = col_peak.reshape(COLS_ALL)
        return (row_scale / jnp.sqrt(row_scale * row_peak + EPS), col_scale / jnp.sqrt(col_scale * col_peak + EPS))

    def forward(vectors):
        shaped = vectors.reshape(SCENARIOS, tile_cols, TILE_WIDTH).astype(jnp.float32)

        def advance(running, scanned):
            block, weights = scanned
            pieces = jnp.einsum('ibj,sbj->sbi', block.astype(jnp.float32), shaped, precision=lax.Precision.HIGHEST)
            return (running, lax.optimization_barrier(jnp.sum(pieces * weights[None, :, None], axis=1)))
        _, images = lax.scan(advance, jnp.zeros((), jnp.float32), (blocks, factor))
        return jnp.transpose(images, (1, 0, 2)).reshape(SCENARIOS, ROWS_ALL)

    def backward(vectors):
        shaped = jnp.transpose(vectors.reshape(SCENARIOS, tile_rows, TILE_WIDTH).astype(jnp.float32), (1, 0, 2))

        def advance(running, scanned):
            block, weights, piece = scanned
            pieces = jnp.einsum('ibj,si->sbj', block.astype(jnp.float32), piece, precision=lax.Precision.HIGHEST)
            return (running + pieces * weights[None, :, None], jnp.zeros((), jnp.float32))
        total, _ = lax.scan(advance, jnp.zeros((SCENARIOS, tile_cols, TILE_WIDTH), jnp.float32), (blocks, factor, shaped))
        return total.reshape(SCENARIOS, COLS_ALL)
    row_scale = jnp.ones((ROWS_ALL,), jnp.float32)
    col_scale = jnp.ones((COLS_ALL,), jnp.float32)
    for repeat_index in range(2):
        row_scale, col_scale = sweep_scales(row_scale, col_scale)
    primal_step = step_sizes[0]
    dual_step = step_sizes[1]
    cost_scaled = cost_vector * col_scale[None]
    low_scaled = lower_bound / col_scale
    high_scaled = upper_bound / col_scale
    rhs_scaled = right_side * row_scale[None]
    dual_first = col_scale[None] * backward((y_start * row_scale[None]).astype(jnp.bfloat16))
    x_next = jnp.clip(x_start - primal_step * (cost_scaled - dual_first), low_scaled[None], high_scaled[None])
    image_first = row_scale[None] * forward((x_start * col_scale[None]).astype(jnp.bfloat16))
    image_next = row_scale[None] * forward((x_next * col_scale[None]).astype(jnp.bfloat16))
    inequality = (row_kind == 1)[None, :]
    dual_trial = y_start + dual_step * (rhs_scaled - (2.0 * image_next - image_first))
    y_next = jnp.where(inequality, jnp.maximum(dual_trial, 0.0), dual_trial)
    dual_second = col_scale[None] * backward((y_next * row_scale[None]).astype(jnp.bfloat16))
    x_mean = 0.5 * (x_start + x_next)
    y_mean = 0.5 * (y_start + y_next)
    image_mean = 0.5 * (image_first + image_next)
    reduced = cost_scaled - 0.5 * (dual_first + dual_second)
    violation = rhs_scaled - image_mean
    violation = jnp.where(inequality, jnp.maximum(violation, 0.0), violation)
    primal_residual = lax.optimization_barrier(jnp.sum(violation * violation, axis=1)) / ROWS_ALL
    rows_part = lax.optimization_barrier(jnp.sum(rhs_scaled * y_mean, axis=1))
    bound_part = lax.optimization_barrier(jnp.sum(low_scaled[None] * jnp.maximum(reduced, 0.0) - high_scaled[None] * jnp.maximum(-reduced, 0.0), axis=1))
    duality_gap = (lax.optimization_barrier(jnp.sum(cost_scaled * x_mean, axis=1)) - rows_part - bound_part) / COLS_ALL
    move_primal = lax.optimization_barrier(jnp.sum((x_next - x_start) ** 2, axis=1)) / COLS_ALL
    move_dual = lax.optimization_barrier(jnp.sum((y_next - y_start) ** 2, axis=1)) / ROWS_ALL
    measures = jnp.stack([primal_residual, duality_gap, move_dual])
    return (x_next, y_next, measures, move_primal)
```

```python
import jax
import jax.numpy as jnp
from jax import lax
from jax.experimental import pallas as pl
from jax.experimental.pallas import tpu as pltpu
from jax.sharding import PartitionSpec as P

EPS = 1e-06
MESH = pl.DeviceIdType.MESH
F32 = jnp.float32
BF16 = jnp.bfloat16

Z_HIGH, Y_SIZE, CORES = 4, 8, 2
X_SIZE, Z_LOW = 4, 3
LANE = 128
TILE = 256


def ring_distance(offset, size):
    return min(offset, size - offset)


def kernel(
    values_in,
    scale_ref,
    occupancy_ref,
    kind_ref,
    rhs_in,
    cost_in,
    low_ref,
    high_ref,
    x_in,
    y_in,
    step_ref,
    x_out,
    y_out,
    measures_ref,
    move_ref,
    values,
    rhs,
    cost,
    x_start,
    y_start,
    magnitude,
    col_peak,
    row_peak,
    col_first,
    row_first,
    col_second,
    col_scale,
    row_scale,
    part,
    half_in,
    half,
    group_in,
    high_slots,
    dual_first,
    x_full,
    image,
    image_in,
    image_first,
    y_full,
    y_sums,
    sums_cols,
    sums_rows,
    send,
    recv,
    local,
):
    scenarios = x_full.shape[0]
    rows_here, cols_here = values.shape
    row_blocks, col_blocks = rows_here // LANE, cols_here // LANE
    per_tile = TILE // LANE
    group_rows = scenarios // (CORES * Y_SIZE)
    half_rows = scenarios // CORES
    chunk_rows = scenarios // X_SIZE
    chunk_cols = rows_here // Z_LOW
    rows_total = float(rows_here * Z_HIGH * Y_SIZE * CORES)
    cols_total = float(cols_here * X_SIZE * Z_LOW)

    rank, column = lax.axis_index("rows"), lax.axis_index("cols")
    core = lax.rem(rank, CORES)
    y = lax.rem(lax.div(rank, CORES), Y_SIZE)
    z_high = lax.div(rank, CORES * Y_SIZE)
    x = lax.div(column, Z_LOW)
    z_low = lax.rem(column, Z_LOW)
    group = core * Y_SIZE + y

    def at_rows(z_at, y_at, core_at):
        return ((z_at * Y_SIZE + y_at) * CORES + core_at, column)

    def at_cols(x_at, low_at):
        return (rank, x_at * Z_LOW + low_at)

    def shift(index, offset, size):
        return lax.rem(index + offset + size, size)

    y_offsets = sorted(range(1, Y_SIZE), key=lambda k: -ring_distance(k, Y_SIZE))
    plane_offsets = [
        (dy, dc) for dy in range(Y_SIZE) for dc in range(CORES) if (dy, dc) != (0, 0)
    ]
    plane_offsets.sort(key=lambda o: -ring_distance(o[0], Y_SIZE))
    z_offsets = sorted(range(1, Z_HIGH), key=lambda k: -ring_distance(k, Z_HIGH))
    col_offsets = [
        (dx, dl) for dx in range(X_SIZE) for dl in range(Z_LOW) if (dx, dl) != (0, 0)
    ]
    col_offsets.sort(key=lambda o: -(ring_distance(o[0], X_SIZE) + (o[1] != 0)))

    def plane_at(offset, sign):
        return shift(y, sign * offset[0], Y_SIZE), shift(core, sign * offset[1], CORES)

    def cols_at(offset, sign):
        return shift(x, sign * offset[0], X_SIZE), shift(z_low, sign * offset[1], Z_LOW)

    plane_to = [at_rows(z_high, *plane_at(o, 1)) for o in plane_offsets]
    z_to = [at_rows(shift(z_high, k, Z_HIGH), y, core) for k in z_offsets]
    y_to = [at_rows(z_high, shift(y, k, Y_SIZE), core) for k in y_offsets]
    cols_to = [at_cols(*cols_at(o, 1)) for o in col_offsets]
    partner = at_rows(z_high, y, 1 - core)

    started = []
    used = [0]

    def reserve(count):
        base = used[0]
        used[0] += count
        return base

    def copy(source, target, slot, device):
        return pltpu.make_async_remote_copy(
            src_ref=source,
            dst_ref=target,
            send_sem=send.at[slot],
            recv_sem=recv.at[slot],
            device_id=device,
            device_id_type=MESH,
        )

    def put(source, target, slot, device):
        moved = copy(source, target, slot, device)
        moved.start()
        started.append(moved)

    def arrived(target, slot, device):
        copy(target, target, slot, device).wait_recv()

    def spread(source, slots, peers):
        base = reserve(len(peers))
        for k, device in enumerate(peers):
            put(source, slots.at[k], base + k, device)
        return base

    def collect(slots, base, peers):
        for k, device in enumerate(peers):
            arrived(slots.at[k], base + k, device)

    def block(index):
        return slice(index * LANE, (index + 1) * LANE)

    loads = [
        pltpu.make_async_copy(source, target, local.at[k])
        for k, (source, target) in enumerate(
            [(values_in, values), (y_in, y_start), (x_in, x_start), (cost_in, cost), (rhs_in, rhs)]
        )
    ]
    for load in loads:
        load.start()
    barrier = pltpu.get_barrier_semaphore()
    everyone = plane_to + z_to + cols_to
    for device in everyone:
        pl.semaphore_signal(barrier, inc=1, device_id=device, device_id_type=MESH)

    factor = [
        [
            scale_ref[a, b] * occupancy_ref[a, b].astype(F32)
            for b in range(cols_here // TILE)
        ]
        for a in range(rows_here // TILE)
    ]

    def fold(array):
        return jnp.max(array.reshape(LANE // 8, 8, LANE), axis=0)

    for ref in (col_peak, row_peak):
        ref[...] = jnp.zeros_like(ref)
    loads[0].wait()
    col_best = [None] * col_blocks
    for q in range(row_blocks):
        across = None
        for l in range(col_blocks):
            entries = jnp.abs(values[block(q), block(l)].astype(F32)) * factor[q // per_tile][l // per_tile]
            magnitude[block(q), block(l)] = entries
            across = entries if across is None else jnp.maximum(across, entries)
            best = fold(entries)
            col_best[l] = best if q == 0 else jnp.maximum(col_best[l], best)
        row_peak[0, q : q + 1, :] = jnp.max(across.T, axis=0, keepdims=True)
    for l in range(col_blocks):
        col_peak[0, l : l + 1, :] = jnp.max(col_best[l], axis=0, keepdims=True)

    pl.semaphore_wait(barrier, len(everyone))
    plane_base = spread(col_peak.at[0], col_first.at[0], plane_to)
    row_base = spread(row_peak.at[0], row_first.at[0], cols_to)

    def best_of(own, slots, count):
        best = own
        for k in range(count):
            best = jnp.maximum(best, slots[k])
        return best

    collect(col_first.at[0], plane_base, plane_to)
    col_peak[1] = best_of(col_peak[0], col_first.at[0], len(plane_to))
    z_base = spread(col_peak.at[1], col_second.at[0], z_to)

    collect(row_first.at[0], row_base, cols_to)
    row_scale[0] = 1.0 / jnp.sqrt(best_of(row_peak[0], row_first.at[0], len(cols_to)) + EPS)

    for q in range(row_blocks):
        down = jnp.broadcast_to(row_scale[0, q : q + 1, :], (LANE, LANE)).T
        for l in range(col_blocks):
            best = fold(magnitude[block(q), block(l)] * down)
            col_best[l] = best if q == 0 else jnp.maximum(col_best[l], best)
    for l in range(col_blocks):
        col_peak[2, l : l + 1, :] = jnp.max(col_best[l], axis=0, keepdims=True)
    plane_base = spread(col_peak.at[2], col_first.at[1], plane_to)

    collect(col_second.at[0], z_base, z_to)
    col_scale[0] = 1.0 / jnp.sqrt(best_of(col_peak[1], col_second.at[0], len(z_to)) + EPS)

    for q in range(row_blocks):
        across = None
        for l in range(col_blocks):
            entries = magnitude[block(q), block(l)] * col_scale[0, l : l + 1, :]
            across = entries if across is None else jnp.maximum(across, entries)
        row_peak[1, q : q + 1, :] = jnp.max(across.T, axis=0, keepdims=True)
    row_base = spread(row_peak.at[1], row_first.at[1], cols_to)

    collect(col_first.at[1], plane_base, plane_to)
    col_peak[3] = best_of(col_peak[2], col_first.at[1], len(plane_to))
    z_base = spread(col_peak.at[3], col_second.at[1], z_to)

    loads[1].wait()
    collect(row_first.at[1], row_base, cols_to)
    peak = best_of(row_peak[1], row_first.at[1], len(cols_to))
    row_scale[1] = row_scale[0] / jnp.sqrt(row_scale[0] * peak + EPS)

    own_half = pl.ds(pl.multiple_of(core * half_rows, half_rows), half_rows)
    other_half = pl.ds(pl.multiple_of((1 - core) * half_rows, half_rows), half_rows)

    def group_of(core_at, y_at):
        start = (core_at * Y_SIZE + y_at) * group_rows
        return pl.ds(pl.multiple_of(start, group_rows), group_rows)

    def in_half(y_at):
        return pl.ds(pl.multiple_of(y_at * group_rows, group_rows), group_rows)

    def backward(duals, step):
        scaled = [
            jnp.concatenate(
                [
                    duals[:, block(q)] * row_scale[1, q : q + 1, :]
                    for q in range(a * per_tile, (a + 1) * per_tile)
                ],
                axis=1,
            ).astype(BF16)
            for a in range(rows_here // TILE)
        ]
        for b in range(cols_here // TILE):
            at_b = slice(b * TILE, (b + 1) * TILE)
            total = None
            for a in range(rows_here // TILE):
                term = factor[a][b] * jnp.dot(
                    scaled[a],
                    values[a * TILE : (a + 1) * TILE, at_b],
                    preferred_element_type=F32,
                )
                total = term if total is None else total + term
            part[step, :, at_b] = total
        base = reserve(1)
        put(part.at[step, other_half, :], half_in.at[step], base, partner)
        return base

    def over_y(step, base):
        arrived(half_in.at[step], base, partner)
        half[step] = part[step, own_half, :] + half_in[step]
        base = reserve(len(y_offsets))
        for k, offset in enumerate(y_offsets):
            to = shift(y, offset, Y_SIZE)
            put(half.at[step, in_half(to), :], group_in.at[step, k], base + k, y_to[k])
        return base

    def over_z(step, base):
        for k, device in enumerate(y_to):
            arrived(group_in.at[step, k], base + k, device)
        total = half[step, in_half(y), :]
        for k in range(len(y_to)):
            total = total + group_in[step, k]
        high_slots[step, z_high] = total
        base = reserve(len(z_to))
        for k, device in enumerate(z_to):
            put(high_slots.at[step, z_high], high_slots.at[step, z_high], base + k, device)
        return base

    def z_slots_in(slots, base):
        for k, offset in enumerate(z_offsets):
            arrived(slots.at[shift(z_high, -offset, Z_HIGH)], base + k, z_to[k])
        total = slots[0]
        for k in range(1, Z_HIGH):
            total = total + slots[k]
        return total

    own_rows = pl.ds(pl.multiple_of(x * chunk_rows, chunk_rows), chunk_rows)
    own_cols = pl.ds(pl.multiple_of(z_low * chunk_cols, chunk_cols), chunk_cols)

    def forward(vectors, step):
        scaled = [
            jnp.concatenate(
                [
                    vectors[:, block(l)] * col_scale[1, l : l + 1, :]
                    for l in range(b * per_tile, (b + 1) * per_tile)
                ],
                axis=1,
            ).astype(BF16)
            for b in range(cols_here // TILE)
        ]
        for a in range(rows_here // TILE):
            at_a = slice(a * TILE, (a + 1) * TILE)
            total = None
            for b in range(cols_here // TILE):
                term = factor[a][b] * lax.dot_general(
                    scaled[b],
                    values[at_a, b * TILE : (b + 1) * TILE],
                    (((1,), (1,)), ((), ())),
                    preferred_element_type=F32,
                )
                total = term if total is None else total + term
            image[step, :, at_a] = total

    def over_cols(step):
        base = reserve(len(cols_to))
        for k, offset in enumerate(col_offsets):
            x_at, low_at = cols_at(offset, 1)
            rows = pl.ds(pl.multiple_of(x_at * chunk_rows, chunk_rows), chunk_rows)
            cols = pl.ds(pl.multiple_of(low_at * chunk_cols, chunk_cols), chunk_cols)
            put(image.at[step, rows, cols], image_in.at[step, k], base + k, cols_to[k])
        return base

    def image_sum(step, base):
        for k, device in enumerate(cols_to):
            arrived(image_in.at[step, k], base + k, device)
        total = image[step, own_rows, own_cols]
        for k in range(len(cols_to)):
            total = total + image_in[step, k]
        return total

    half_base = backward(y_start, 0)
    collect(col_second.at[1], z_base, z_to)
    peak = best_of(col_peak[3], col_second.at[1], len(z_to))
    col_scale[1] = col_scale[0] / jnp.sqrt(col_scale[0] * peak + EPS)
    group_base = over_y(0, half_base)
    loads[2].wait()
    forward(x_start, 0)
    first_base = over_cols(0)
    z_base = over_z(0, group_base)
    loads[3].wait()
    loads[4].wait()

    own_group = group_of(core, y)
    primal_step, dual_step = step_ref[0], step_ref[1]

    def of_block(l):
        scale = col_scale[1, l : l + 1, :]
        return (
            x_start[own_group, block(l)],
            cost[own_group, block(l)] * scale,
            low_ref[0:1, block(l)] / scale,
            high_ref[0:1, block(l)] / scale,
        )

    summed = z_slots_in(high_slots.at[0], z_base)
    for l in range(col_blocks):
        old, cost_scaled, low_scaled, high_scaled = of_block(l)
        dual = col_scale[1, l : l + 1, :] * summed[:, block(l)]
        dual_first[:, block(l)] = dual
        new = old - primal_step * (cost_scaled - dual)
        x_full[own_group, block(l)] = jnp.minimum(jnp.maximum(new, low_scaled), high_scaled)

    y_base = reserve(len(y_to))
    relay_base = reserve(Y_SIZE)
    for k, device in enumerate(y_to):
        put(x_full.at[own_group, :], x_full.at[own_group, :], y_base + k, device)
    put(x_full.at[own_group, :], x_full.at[own_group, :], relay_base + Y_SIZE - 1, partner)

    image_first[...] = image_sum(0, first_base)

    for k in reversed(range(len(y_to))):
        rows = group_of(core, shift(y, -y_offsets[k], Y_SIZE))
        arrived(x_full.at[rows, :], y_base + k, y_to[k])
        put(x_full.at[rows, :], x_full.at[rows, :], relay_base + k, partner)
    for k, offset in enumerate(y_offsets + [0]):
        rows = group_of(1 - core, shift(y, -offset, Y_SIZE))
        arrived(x_full.at[rows, :], relay_base + k, partner)

    forward(x_full, 1)
    second_base = over_cols(1)
    x_written = pltpu.make_async_copy(x_full, x_out, local.at[5])
    x_written.start()

    scale = jnp.concatenate(
        [row_scale[1, pl.ds(z_low * (chunk_cols // LANE) + j, 1), :] for j in range(chunk_cols // LANE)],
        axis=1,
    )
    y_old = y_start[own_rows, own_cols]
    rhs_scaled = rhs[own_rows, own_cols] * scale
    inequality = kind_ref[0:1, own_cols] == 1
    first = scale * image_first[...]
    second = scale * image_sum(1, second_base)
    trial = y_old + dual_step * (rhs_scaled - (2.0 * second - first))
    y_new = jnp.where(inequality, jnp.maximum(trial, 0.0), trial)
    y_full[own_rows, own_cols] = y_new
    y_base = reserve(len(cols_to))
    for k, device in enumerate(cols_to):
        put(y_full.at[own_rows, own_cols], y_full.at[own_rows, own_cols], y_base + k, device)

    def on_lanes(terms, first_row):
        sums = jnp.sum(terms, axis=1, keepdims=True)
        shape = (terms.shape[0], scenarios)
        lanes = lax.broadcasted_iota(jnp.int32, shape, 1)
        rows = lax.broadcasted_iota(jnp.int32, shape, 0)
        spread_out = jnp.where(lanes == rows + first_row, jnp.broadcast_to(sums, shape), 0.0)
        return jnp.sum(spread_out, axis=0, keepdims=True)

    violation = rhs_scaled - 0.5 * (first + second)
    violation = jnp.where(inequality, jnp.maximum(violation, 0.0), violation)
    y_mean = 0.5 * (y_old + y_new)
    y_sums[z_high] = jnp.zeros(y_sums.shape[1:], F32)
    first_row = x * chunk_rows
    y_sums[z_high, 0:1, :] = on_lanes(violation * violation, first_row)
    y_sums[z_high, 1:2, :] = on_lanes(rhs_scaled * y_mean, first_row)
    y_sums[z_high, 2:3, :] = on_lanes((y_new - y_old) * (y_new - y_old), first_row)
    sums_base = reserve(len(z_to))
    for k, device in enumerate(z_to):
        put(y_sums.at[z_high], y_sums.at[z_high], sums_base + k, device)

    for k, offset in enumerate(col_offsets):
        x_at, low_at = cols_at(offset, -1)
        rows = pl.ds(pl.multiple_of(x_at * chunk_rows, chunk_rows), chunk_rows)
        cols = pl.ds(pl.multiple_of(low_at * chunk_cols, chunk_cols), chunk_cols)
        arrived(y_full.at[rows, cols], y_base + k, cols_to[k])

    half_base = backward(y_full, 1)
    y_written = pltpu.make_async_copy(y_full, y_out, local.at[6])
    y_written.start()
    group_base = over_y(1, half_base)
    first_row = group * group_rows
    products = moves = None
    for l in range(col_blocks):
        old, cost_scaled, _, _ = of_block(l)
        new = x_full[own_group, block(l)]
        product = cost_scaled * (0.5 * (old + new))
        move = (new - old) * (new - old)
        products = product if products is None else products + product
        moves = move if moves is None else moves + move
    products, moves = on_lanes(products, first_row), on_lanes(moves, first_row)
    z_base = over_z(1, group_base)
    rows_sum = z_slots_in(y_sums, sums_base)
    summed = z_slots_in(high_slots.at[1], z_base)
    bounds = None
    for l in range(col_blocks):
        _, cost_scaled, low_scaled, high_scaled = of_block(l)
        dual = col_scale[1, l : l + 1, :] * summed[:, block(l)]
        reduced = cost_scaled - 0.5 * (dual_first[:, block(l)] + dual)
        bound = low_scaled * jnp.maximum(reduced, 0.0) - high_scaled * jnp.maximum(-reduced, 0.0)
        bounds = bound if bounds is None else bounds + bound
    sums_cols[column] = rows_sum
    sums_cols[column, 3:4, :] = products
    sums_cols[column, 4:5, :] = on_lanes(bounds, first_row)
    sums_cols[column, 5:6, :] = moves

    base = reserve(len(cols_to))
    for k, device in enumerate(cols_to):
        put(sums_cols.at[column], sums_cols.at[column], base + k, device)
    for k, offset in enumerate(col_offsets):
        x_at, low_at = cols_at(offset, -1)
        arrived(sums_cols.at[x_at * Z_LOW + low_at], base + k, cols_to[k])
    total = sums_cols[0]
    for k in range(1, X_SIZE * Z_LOW):
        total = total + sums_cols[k]
    sums_rows[group] = total
    base = reserve(len(plane_to))
    for k, device in enumerate(plane_to):
        put(sums_rows.at[group], sums_rows.at[group], base + k, device)
    for k, offset in enumerate(plane_offsets):
        y_at, core_at = plane_at(offset, -1)
        arrived(sums_rows.at[core_at * Y_SIZE + y_at], base + k, plane_to[k])
    total = sums_rows[0]
    for k in range(1, CORES * Y_SIZE):
        total = total + sums_rows[k]

    measures_ref[0:1, :] = total[0:1, :] / rows_total
    measures_ref[1:2, :] = (total[3:4, :] - total[1:2, :] - total[4:5, :]) / cols_total
    measures_ref[2:3, :] = total[2:3, :] / rows_total
    move_ref[...] = total[5:6, :] / cols_total
    x_written.wait()
    y_written.wait()
    for moved in started:
        moved.wait_send()


def per_device(
    values,
    tile_scale,
    occupancy,
    row_kind,
    right_side,
    cost_vector,
    lower_bound,
    upper_bound,
    x_start,
    y_start,
    step_sizes,
):
    rows_here, cols_here = values.shape
    scenarios = x_start.shape[0]
    plane, cols_size = CORES * Y_SIZE, X_SIZE * Z_LOW
    group_rows, half_rows = scenarios // plane, scenarios // CORES
    chunk = (scenarios // X_SIZE, rows_here // Z_LOW)
    semaphores = 2 * (plane + Z_HIGH + cols_size - 3) + 2 * (1 + Y_SIZE + Z_HIGH - 2)
    semaphores += 2 * Y_SIZE - 1 + 3 * (cols_size - 1) + Z_HIGH - 1 + cols_size - 1 + plane - 1
    vmem, smem, anywhere = (
        pl.BlockSpec(memory_space=space) for space in (pltpu.VMEM, pltpu.SMEM, pl.ANY)
    )
    x_next, y_next, measures, move = pl.pallas_call(
        kernel,
        out_shape=(
            jax.ShapeDtypeStruct((scenarios, cols_here), F32),
            jax.ShapeDtypeStruct((scenarios, rows_here), F32),
            jax.ShapeDtypeStruct((3, scenarios), F32),
            jax.ShapeDtypeStruct((1, scenarios), F32),
        ),
        in_specs=[
            anywhere,
            smem,
            smem,
            vmem,
            anywhere,
            anywhere,
            vmem,
            vmem,
            anywhere,
            anywhere,
            smem,
        ],
        out_specs=(anywhere, anywhere, vmem, vmem),
        scratch_shapes=[
            pltpu.VMEM((rows_here, cols_here), BF16),
            pltpu.VMEM((scenarios, rows_here), F32),
            pltpu.VMEM((scenarios, cols_here), F32),
            pltpu.VMEM((scenarios, cols_here), F32),
            pltpu.VMEM((scenarios, rows_here), F32),
            pltpu.VMEM((rows_here, cols_here), F32),
            pltpu.VMEM((4, 8, LANE), F32),
            pltpu.VMEM((2, 8, LANE), F32),
            pltpu.VMEM((2, plane - 1, 8, LANE), F32),
            pltpu.VMEM((2, cols_size - 1, 8, LANE), F32),
            pltpu.VMEM((2, Z_HIGH - 1, 8, LANE), F32),
            pltpu.VMEM((2, 8, LANE), F32),
            pltpu.VMEM((2, 8, LANE), F32),
            pltpu.VMEM((2, scenarios, cols_here), F32),
            pltpu.VMEM((2, half_rows, cols_here), F32),
            pltpu.VMEM((2, half_rows, cols_here), F32),
            pltpu.VMEM((2, Y_SIZE - 1, group_rows, cols_here), F32),
            pltpu.VMEM((2, Z_HIGH, group_rows, cols_here), F32),
            pltpu.VMEM((group_rows, cols_here), F32),
            pltpu.VMEM((scenarios, cols_here), F32),
            pltpu.VMEM((2, scenarios, rows_here), F32),
            pltpu.VMEM((2, cols_size - 1) + chunk, F32),
            pltpu.VMEM(chunk, F32),
            pltpu.VMEM((scenarios, rows_here), F32),
            pltpu.VMEM((Z_HIGH, 8, scenarios), F32),
            pltpu.VMEM((cols_size, 8, scenarios), F32),
            pltpu.VMEM((plane, 8, scenarios), F32),
            pltpu.SemaphoreType.DMA((semaphores,)),
            pltpu.SemaphoreType.DMA((semaphores,)),
            pltpu.SemaphoreType.DMA((7,)),
        ],
        compiler_params=pltpu.CompilerParams(
            collective_id=0, has_side_effects=True, vmem_limit_bytes=32 << 20
        ),
    )(
        values,
        tile_scale,
        occupancy,
        row_kind.reshape(1, -1),
        right_side,
        cost_vector,
        lower_bound.reshape(1, -1),
        upper_bound.reshape(1, -1),
        x_start,
        y_start,
        step_sizes,
    )
    return x_next, y_next, measures, move.reshape(-1)


def solution(mesh):
    return jax.shard_map(
        per_device,
        mesh=mesh,
        in_specs=(
            P("rows", "cols"),
            P("rows", "cols"),
            P("rows", "cols"),
            P("rows"),
            P(None, "rows"),
            P(None, "cols"),
            P("cols"),
            P("cols"),
            P(None, "cols"),
            P(None, "rows"),
            P(),
        ),
        out_specs=(P(None, "cols"), P(None, "rows"), P(), P()),
        check_vma=False,
    )
```

```python
import jax
import jax.numpy as jnp
from jax import lax
from jax.experimental import pallas as pl
from jax.experimental.pallas import tpu as pltpu
from jax.sharding import PartitionSpec as P

EPS = 1e-06
MESH = pl.DeviceIdType.MESH
F32 = jnp.float32
BF16 = jnp.bfloat16

Z_HIGH, Y_SIZE, CORES = 4, 8, 2
X_SIZE, Z_LOW = 4, 3
LANE = 128
TILE = 256


def ring_distance(offset, size):
    return min(offset, size - offset)


def kernel(
    values_in,
    scale_in,
    occupancy_in,
    kind_in,
    rhs_in,
    cost_in,
    low_in,
    high_in,
    x_in,
    y_in,
    step_in,
    x_out,
    y_out,
    measures_ref,
    move_ref,
    values,
    rhs,
    cost,
    x_start,
    y_start,
    scale_ref,
    occupancy_ref,
    kind_ref,
    low_ref,
    high_ref,
    step_ref,
    magnitude,
    col_peak,
    row_peak,
    col_first,
    row_first,
    col_second,
    col_scale,
    row_scale,
    scaled_duals,
    half_out,
    half_in,
    half,
    group_in,
    high_slots,
    dual_first,
    x_full,
    image,
    image_in,
    image_first,
    y_full,
    bounds_scaled,
    y_sums,
    early_cols,
    early_rows,
    late_cols,
    late_rows,
    send,
    recv,
    local,
):
    scenarios = x_full.shape[0]
    rows_here, cols_here = values.shape
    row_blocks, col_blocks = rows_here // LANE, cols_here // LANE
    per_tile = TILE // LANE
    group_rows = scenarios // (CORES * Y_SIZE)
    half_rows = scenarios // CORES
    chunk_rows = scenarios // X_SIZE
    chunk_cols = rows_here // Z_LOW
    rows_total = float(rows_here * Z_HIGH * Y_SIZE * CORES)
    cols_total = float(cols_here * X_SIZE * Z_LOW)

    rank, column = lax.axis_index("rows"), lax.axis_index("cols")
    core = lax.rem(rank, CORES)
    y = lax.rem(lax.div(rank, CORES), Y_SIZE)
    z_high = lax.div(rank, CORES * Y_SIZE)
    x = lax.div(column, Z_LOW)
    z_low = lax.rem(column, Z_LOW)
    group = core * Y_SIZE + y

    def at_rows(z_at, y_at, core_at):
        return ((z_at * Y_SIZE + y_at) * CORES + core_at, column)

    def at_cols(x_at, low_at):
        return (rank, x_at * Z_LOW + low_at)

    def shift(index, offset, size):
        return lax.rem(index + offset + size, size)

    y_offsets = sorted(range(1, Y_SIZE), key=lambda k: -ring_distance(k, Y_SIZE))
    plane_offsets = [
        (dy, dc) for dy in range(Y_SIZE) for dc in range(CORES) if (dy, dc) != (0, 0)
    ]
    plane_offsets.sort(key=lambda o: -ring_distance(o[0], Y_SIZE))
    z_offsets = sorted(range(1, Z_HIGH), key=lambda k: -ring_distance(k, Z_HIGH))
    col_offsets = [
        (dx, dl) for dx in range(X_SIZE) for dl in range(Z_LOW) if (dx, dl) != (0, 0)
    ]
    col_offsets.sort(key=lambda o: -(ring_distance(o[0], X_SIZE) + (o[1] != 0)))

    def plane_at(offset, sign):
        return shift(y, sign * offset[0], Y_SIZE), shift(core, sign * offset[1], CORES)

    def cols_at(offset, sign):
        return shift(x, sign * offset[0], X_SIZE), shift(z_low, sign * offset[1], Z_LOW)

    plane_to = [at_rows(z_high, *plane_at(o, 1)) for o in plane_offsets]
    z_to = [at_rows(shift(z_high, k, Z_HIGH), y, core) for k in z_offsets]
    y_to = [at_rows(z_high, shift(y, k, Y_SIZE), core) for k in y_offsets]
    cols_to = [at_cols(*cols_at(o, 1)) for o in col_offsets]
    partner = at_rows(z_high, y, 1 - core)

    started = []
    used = [0]

    def reserve(count):
        base = used[0]
        used[0] += count
        return base

    def copy(source, target, slot, device):
        return pltpu.make_async_remote_copy(
            src_ref=source,
            dst_ref=target,
            send_sem=send.at[slot],
            recv_sem=recv.at[slot],
            device_id=device,
            device_id_type=MESH,
        )

    def put(source, target, slot, device):
        moved = copy(source, target, slot, device)
        moved.start()
        started.append(moved)

    def arrived(target, slot, device):
        copy(target, target, slot, device).wait_recv()

    def spread(source, slots, peers):
        base = reserve(len(peers))
        for k, device in enumerate(peers):
            put(source, slots.at[k], base + k, device)
        return base

    def collect(slots, base, peers):
        for k, device in enumerate(peers):
            arrived(slots.at[k], base + k, device)

    def share(slots, own, targets):
        base = reserve(len(targets))
        for k, device in enumerate(targets):
            put(slots.at[own], slots.at[own], base + k, device)
        return base

    def added(slots, sources, base, targets):
        for k, device in enumerate(targets):
            arrived(slots.at[sources[k]], base + k, device)
        total = slots[0]
        for k in range(1, slots.shape[0]):
            total = total + slots[k]
        return total

    def block(index):
        return slice(index * LANE, (index + 1) * LANE)

    loads = [
        pltpu.make_async_copy(source, target, local.at[k])
        for k, (source, target) in enumerate(
            [
                (scale_in, scale_ref),
                (occupancy_in, occupancy_ref),
                (values_in, values),
                (y_in, y_start),
                (x_in, x_start),
                (cost_in, cost),
                (rhs_in, rhs),
                (low_in, low_ref),
                (high_in, high_ref),
                (step_in, step_ref),
            ]
            + [(kind_in.at[block(q)], kind_ref.at[q]) for q in range(row_blocks)]
        )
    ]
    for load in loads:
        load.start()
    barrier = pltpu.get_barrier_semaphore()
    everyone = plane_to + z_to + cols_to
    for device in everyone:
        pl.semaphore_signal(barrier, inc=1, device_id=device, device_id_type=MESH)
    loads[0].wait()
    loads[1].wait()

    factor = [
        [
            scale_ref[b, a] * occupancy_ref[b, a].astype(F32)
            for b in range(cols_here // TILE)
        ]
        for a in range(rows_here // TILE)
    ]

    def fold(array):
        return jnp.max(array.reshape(LANE // 8, 8, LANE), axis=0)

    loads[2].wait()
    col_best = [None] * col_blocks
    for q in range(row_blocks):
        across = None
        for l in range(col_blocks):
            entries = jnp.abs(values[block(q), block(l)].astype(F32)) * factor[q // per_tile][l // per_tile]
            magnitude[block(q), block(l)] = entries
            across = entries if across is None else jnp.maximum(across, entries)
            best = fold(entries)
            col_best[l] = best if q == 0 else jnp.maximum(col_best[l], best)
        row_peak[0, q : q + 1, :] = jnp.max(across.T, axis=0, keepdims=True)
    for l in range(col_blocks):
        col_peak[0, l : l + 1, :] = jnp.max(col_best[l], axis=0, keepdims=True)

    pl.semaphore_wait(barrier, len(everyone))
    plane_base = spread(col_peak.at[0], col_first.at[0], plane_to)
    row_base = spread(row_peak.at[0], row_first.at[0], cols_to)

    def best_of(own, slots, count):
        best = own
        for k in range(count):
            best = jnp.maximum(best, slots[k])
        return best

    collect(col_first.at[0], plane_base, plane_to)
    col_peak[1] = best_of(col_peak[0], col_first.at[0], len(plane_to))
    z_base = spread(col_peak.at[1], col_second.at[0], z_to)

    collect(row_first.at[0], row_base, cols_to)
    row_scale[0] = 1.0 / jnp.sqrt(best_of(row_peak[0], row_first.at[0], len(cols_to)) + EPS)

    for q in range(row_blocks):
        down = jnp.broadcast_to(row_scale[0, q : q + 1, :], (LANE, LANE)).T
        for l in range(col_blocks):
            best = fold(magnitude[block(q), block(l)] * down)
            col_best[l] = best if q == 0 else jnp.maximum(col_best[l], best)
    for l in range(col_blocks):
        col_peak[2, l : l + 1, :] = jnp.max(col_best[l], axis=0, keepdims=True)
    plane_base = spread(col_peak.at[2], col_first.at[1], plane_to)

    collect(col_second.at[0], z_base, z_to)
    col_scale[0] = 1.0 / jnp.sqrt(best_of(col_peak[1], col_second.at[0], len(z_to)) + EPS)

    for q in range(row_blocks):
        across = None
        for l in range(col_blocks):
            entries = magnitude[block(q), block(l)] * col_scale[0, l : l + 1, :]
            across = entries if across is None else jnp.maximum(across, entries)
        row_peak[1, q : q + 1, :] = jnp.max(across.T, axis=0, keepdims=True)
    row_base = spread(row_peak.at[1], row_first.at[1], cols_to)

    collect(col_first.at[1], plane_base, plane_to)
    col_peak[3] = best_of(col_peak[2], col_first.at[1], len(plane_to))
    z_base = spread(col_peak.at[3], col_second.at[1], z_to)

    loads[3].wait()
    collect(row_first.at[1], row_base, cols_to)
    peak = best_of(row_peak[1], row_first.at[1], len(cols_to))
    row_scale[1] = row_scale[0] / jnp.sqrt(row_scale[0] * peak + EPS)

    own_half = pl.ds(pl.multiple_of(core * half_rows, half_rows), half_rows)
    other_half = pl.ds(pl.multiple_of((1 - core) * half_rows, half_rows), half_rows)

    def group_of(core_at, y_at):
        start = (core_at * Y_SIZE + y_at) * group_rows
        return pl.ds(pl.multiple_of(start, group_rows), group_rows)

    def in_half(y_at):
        return pl.ds(pl.multiple_of(y_at * group_rows, group_rows), group_rows)

    def backward(duals, step):
        scaled = [
            jnp.concatenate(
                [
                    duals[:, block(q)] * row_scale[1, q : q + 1, :]
                    for q in range(a * per_tile, (a + 1) * per_tile)
                ],
                axis=1,
            ).astype(BF16)
            for a in range(rows_here // TILE)
        ]
        for a in range(rows_here // TILE):
            scaled_duals[:, a * TILE : (a + 1) * TILE] = scaled[a]

        def product(rows, target):
            for b in range(cols_here // TILE):
                at_b = slice(b * TILE, (b + 1) * TILE)
                total = None
                for a in range(rows_here // TILE):
                    at_a = slice(a * TILE, (a + 1) * TILE)
                    term = factor[a][b] * jnp.dot(
                        scaled_duals[rows, at_a], values[at_a, at_b], preferred_element_type=F32
                    )
                    total = term if total is None else total + term
                target[step, :, at_b] = total

        product(other_half, half_out)
        base = reserve(1)
        put(half_out.at[step], half_in.at[step], base, partner)
        product(own_half, half)
        return base

    def over_y(step, base):
        arrived(half_in.at[step], base, partner)
        half[step] = half[step] + half_in[step]
        base = reserve(len(y_offsets))
        for k, offset in enumerate(y_offsets):
            to = shift(y, offset, Y_SIZE)
            put(half.at[step, in_half(to), :], group_in.at[step, k], base + k, y_to[k])
        return base

    def over_z(step, base):
        for k, device in enumerate(y_to):
            arrived(group_in.at[step, k], base + k, device)
        total = half[step, in_half(y), :]
        for k in range(len(y_to)):
            total = total + group_in[step, k]
        high_slots[step, z_high] = total
        base = reserve(len(z_to))
        for k, device in enumerate(z_to):
            put(high_slots.at[step, z_high], high_slots.at[step, z_high], base + k, device)
        return base

    def z_slots_in(slots, base):
        for k, offset in enumerate(z_offsets):
            arrived(slots.at[shift(z_high, -offset, Z_HIGH)], base + k, z_to[k])
        total = slots[0]
        for k in range(1, Z_HIGH):
            total = total + slots[k]
        return total

    own_rows = pl.ds(pl.multiple_of(x * chunk_rows, chunk_rows), chunk_rows)
    pieces = chunk_cols // LANE

    def forward(vectors, step):
        scaled = [
            jnp.concatenate(
                [
                    vectors[:, block(l)] * col_scale[1, l : l + 1, :]
                    for l in range(b * per_tile, (b + 1) * per_tile)
                ],
                axis=1,
            ).astype(BF16)
            for b in range(cols_here // TILE)
        ]
        for a in range(rows_here // TILE):
            at_a = slice(a * TILE, (a + 1) * TILE)
            total = None
            for b in range(cols_here // TILE):
                term = factor[a][b] * lax.dot_general(
                    scaled[b],
                    values[at_a, b * TILE : (b + 1) * TILE],
                    (((1,), (1,)), ((), ())),
                    preferred_element_type=F32,
                )
                total = term if total is None else total + term
            image[step, :, at_a] = total

    def rows_of(x_at):
        return pl.ds(pl.multiple_of(x_at * chunk_rows, chunk_rows), chunk_rows)

    def lanes_of(low_at, piece):
        start = low_at * chunk_cols + piece * LANE
        return pl.ds(pl.multiple_of(start, LANE), LANE)

    def over_cols(step, piece):
        base = reserve(len(cols_to))
        for k, offset in enumerate(col_offsets):
            x_at, low_at = cols_at(offset, 1)
            source = image.at[step, rows_of(x_at), lanes_of(low_at, piece)]
            put(source, image_in.at[step, piece, k], base + k, cols_to[k])
        return base

    def image_sum(step, piece, base):
        for k, device in enumerate(cols_to):
            arrived(image_in.at[step, piece, k], base + k, device)
        total = image[step, own_rows, lanes_of(z_low, piece)]
        for k in range(len(cols_to)):
            total = total + image_in[step, piece, k]
        return total

    half_base = backward(y_start, 0)
    collect(col_second.at[1], z_base, z_to)
    peak = best_of(col_peak[3], col_second.at[1], len(z_to))
    col_scale[1] = col_scale[0] / jnp.sqrt(col_scale[0] * peak + EPS)
    group_base = over_y(0, half_base)
    loads[4].wait()
    forward(x_start, 0)
    z_base = over_z(0, group_base)
    first_bases = [over_cols(0, piece) for piece in range(pieces)]
    for load in loads[5:]:
        load.wait()

    own_group = group_of(core, y)
    primal_step, dual_step = step_ref[0], step_ref[1]

    for l in range(col_blocks):
        col = col_scale[1, l : l + 1, :]
        wide = (group_rows, LANE)
        bounds_scaled[0, :, block(l)] = cost[own_group, block(l)] * col
        bounds_scaled[1, :, block(l)] = jnp.broadcast_to(low_ref[0:1, block(l)] / col, wide)
        bounds_scaled[2, :, block(l)] = jnp.broadcast_to(high_ref[0:1, block(l)] / col, wide)

    summed = z_slots_in(high_slots.at[0], z_base)
    for l in range(col_blocks):
        old = x_start[own_group, block(l)]
        cost_scaled, low_scaled, high_scaled = (bounds_scaled[k, :, block(l)] for k in range(3))
        dual = col_scale[1, l : l + 1, :] * summed[:, block(l)]
        dual_first[:, block(l)] = dual
        new = old - primal_step * (cost_scaled - dual)
        x_full[own_group, block(l)] = jnp.minimum(jnp.maximum(new, low_scaled), high_scaled)

    y_base = reserve(len(y_to))
    relay_base = reserve(Y_SIZE)
    for k, device in enumerate(y_to):
        put(x_full.at[own_group, :], x_full.at[own_group, :], y_base + k, device)
    put(x_full.at[own_group, :], x_full.at[own_group, :], relay_base + Y_SIZE - 1, partner)

    for piece in range(pieces):
        image_first[:, block(piece)] = image_sum(0, piece, first_bases[piece])

    for k in reversed(range(len(y_to))):
        rows = group_of(core, shift(y, -y_offsets[k], Y_SIZE))
        arrived(x_full.at[rows, :], y_base + k, y_to[k])
        put(x_full.at[rows, :], x_full.at[rows, :], relay_base + k, partner)
    for k, offset in enumerate(y_offsets + [0]):
        rows = group_of(1 - core, shift(y, -offset, Y_SIZE))
        arrived(x_full.at[rows, :], relay_base + k, partner)

    forward(x_full, 1)
    second_bases = [over_cols(1, piece) for piece in range(pieces)]
    x_written = pltpu.make_async_copy(x_full, x_out, local.at[len(loads)])
    x_written.start()

    y_bases = []
    violations = products = moves = None

    def add(total, term):
        return term if total is None else total + term

    for piece in range(pieces):
        lanes = lanes_of(z_low, piece)
        line = pl.ds(z_low * pieces + piece, 1)
        scale = row_scale[1, line, :]
        y_old = y_start[own_rows, lanes]
        rhs_scaled = rhs[own_rows, lanes] * scale
        inequality = kind_ref[line, :] == 1
        first = scale * image_first[:, block(piece)]
        second = scale * image_sum(1, piece, second_bases[piece])
        trial = y_old + dual_step * (rhs_scaled - (2.0 * second - first))
        y_new = jnp.where(inequality, jnp.maximum(trial, 0.0), trial)
        y_full[own_rows, lanes] = y_new
        base = reserve(len(cols_to))
        for k, device in enumerate(cols_to):
            put(y_full.at[own_rows, lanes], y_full.at[own_rows, lanes], base + k, device)
        y_bases.append(base)
        violation = rhs_scaled - 0.5 * (first + second)
        violation = jnp.where(inequality, jnp.maximum(violation, 0.0), violation)
        violations = add(violations, violation * violation)
        products = add(products, rhs_scaled * (0.5 * (y_old + y_new)))
        moves = add(moves, (y_new - y_old) * (y_new - y_old))

    def on_lanes(terms, first_row):
        sums = jnp.sum(terms, axis=1, keepdims=True)
        shape = (terms.shape[0], scenarios)
        lanes = lax.broadcasted_iota(jnp.int32, shape, 1)
        rows = lax.broadcasted_iota(jnp.int32, shape, 0)
        spread_out = jnp.where(lanes == rows + first_row, jnp.broadcast_to(sums, shape), 0.0)
        return jnp.sum(spread_out, axis=0, keepdims=True)

    first_row = x * chunk_rows
    y_sums[z_high, 0:1, :] = on_lanes(violations, first_row)
    y_sums[z_high, 1:2, :] = on_lanes(products, first_row)
    y_sums[z_high, 2:3, :] = on_lanes(moves, first_row)
    sums_base = share(y_sums, z_high, z_to)

    for piece in range(pieces):
        for k, offset in enumerate(col_offsets):
            x_at, low_at = cols_at(offset, -1)
            target = y_full.at[rows_of(x_at), lanes_of(low_at, piece)]
            arrived(target, y_bases[piece] + k, cols_to[k])

    half_base = backward(y_full, 1)
    y_written = pltpu.make_async_copy(y_full, y_out, local.at[len(loads) + 1])
    y_written.start()
    group_base = over_y(1, half_base)
    first_row = group * group_rows
    products = moves = None
    for l in range(col_blocks):
        old, new = x_start[own_group, block(l)], x_full[own_group, block(l)]
        products = add(products, bounds_scaled[0, :, block(l)] * (0.5 * (old + new)))
        moves = add(moves, (new - old) * (new - old))
    z_from = [shift(z_high, -k, Z_HIGH) for k in z_offsets]
    cols_from = [cols_at(o, -1)[0] * Z_LOW + cols_at(o, -1)[1] for o in col_offsets]
    plane_from = [plane_at(o, -1)[1] * Y_SIZE + plane_at(o, -1)[0] for o in plane_offsets]
    early_cols[column, 3:4, :] = on_lanes(products, first_row)
    early_cols[column, 4:5, :] = on_lanes(moves, first_row)
    early_cols[column, 0:3, :] = added(y_sums, z_from, sums_base, z_to)
    early_base = share(early_cols, column, cols_to)
    z_base = over_z(1, group_base)
    early_rows[group] = added(early_cols, cols_from, early_base, cols_to)
    early_base = share(early_rows, group, plane_to)
    summed = z_slots_in(high_slots.at[1], z_base)
    bounds = None
    for l in range(col_blocks):
        cost_scaled, low_scaled, high_scaled = (bounds_scaled[k, :, block(l)] for k in range(3))
        dual = col_scale[1, l : l + 1, :] * summed[:, block(l)]
        reduced = cost_scaled - 0.5 * (dual_first[:, block(l)] + dual)
        bound = low_scaled * jnp.maximum(reduced, 0.0) - high_scaled * jnp.maximum(-reduced, 0.0)
        bounds = bound if bounds is None else bounds + bound
    late_cols[column] = on_lanes(bounds, first_row)
    base = share(late_cols, column, cols_to)
    late_rows[group] = added(late_cols, cols_from, base, cols_to)
    base = share(late_rows, group, plane_to)
    total = added(early_rows, plane_from, early_base, plane_to)
    measures_ref[0:1, :] = total[0:1, :] / rows_total
    measures_ref[2:3, :] = total[2:3, :] / rows_total
    move_ref[...] = total[4:5, :] / cols_total
    x_written.wait()
    y_written.wait()
    for moved in started[: -len(plane_to)]:
        moved.wait_send()
    bound_total = added(late_rows, plane_from, base, plane_to)
    measures_ref[1:2, :] = (total[3:4, :] - total[1:2, :] - bound_total) / cols_total
    for moved in started[-len(plane_to) :]:
        moved.wait_send()


def write_out(*refs):
    sources, targets, done = refs[:4], refs[4:8], refs[8]
    writes = [pltpu.make_async_copy(sources[k], targets[k], done.at[k]) for k in range(4)]
    for write in writes:
        write.start()
    for write in writes:
        write.wait()


def per_device(
    values,
    tile_scale,
    occupancy,
    row_kind,
    right_side,
    cost_vector,
    lower_bound,
    upper_bound,
    x_start,
    y_start,
    step_sizes,
):
    rows_here, cols_here = values.shape
    scenarios = x_start.shape[0]
    plane, cols_size = CORES * Y_SIZE, X_SIZE * Z_LOW
    row_blocks, col_blocks = rows_here // LANE, cols_here // LANE
    group_rows, half_rows = scenarios // plane, scenarios // CORES
    chunk = (scenarios // X_SIZE, rows_here // Z_LOW)
    semaphores = 2 * (plane + Z_HIGH + cols_size - 3) + 2 * (1 + Y_SIZE + Z_HIGH - 2)
    semaphores += 2 * Y_SIZE - 1 + 3 * (chunk[1] // LANE) * (cols_size - 1) + Z_HIGH - 1 + 2 * (cols_size - 1 + plane - 1)
    vmem, hbm, anywhere = (
        pl.BlockSpec(memory_space=space) for space in (pltpu.VMEM, pltpu.HBM, pl.ANY)
    )
    x_next, y_next, measures, move = pl.pallas_call(
        kernel,
        out_shape=(
            pltpu.VMEM((scenarios, cols_here), F32),
            pltpu.VMEM((scenarios, rows_here), F32),
            pltpu.VMEM((3, scenarios), F32),
            pltpu.VMEM((1, scenarios), F32),
        ),
        in_specs=[hbm] * 11,
        out_specs=(anywhere, anywhere, vmem, vmem),
        scratch_shapes=[
            pltpu.VMEM((rows_here, cols_here), BF16),
            pltpu.VMEM((scenarios, rows_here), F32),
            pltpu.VMEM((scenarios, cols_here), F32),
            pltpu.VMEM((scenarios, cols_here), F32),
            pltpu.VMEM((scenarios, rows_here), F32),
            pltpu.SMEM((cols_here // TILE, rows_here // TILE), F32),
            pltpu.SMEM((cols_here // TILE, rows_here // TILE), jnp.int32),
            pltpu.VMEM((8, LANE), jnp.int32),
            pltpu.VMEM((1, cols_here), F32),
            pltpu.VMEM((1, cols_here), F32),
            pltpu.SMEM((2,), F32),
            pltpu.VMEM((rows_here, cols_here), F32),
            pltpu.VMEM((4, col_blocks, LANE), F32),
            pltpu.VMEM((2, row_blocks, LANE), F32),
            pltpu.VMEM((2, plane - 1, col_blocks, LANE), F32),
            pltpu.VMEM((2, cols_size - 1, row_blocks, LANE), F32),
            pltpu.VMEM((2, Z_HIGH - 1, col_blocks, LANE), F32),
            pltpu.VMEM((2, col_blocks, LANE), F32),
            pltpu.VMEM((2, row_blocks, LANE), F32),
            pltpu.VMEM((scenarios, rows_here), BF16),
            pltpu.VMEM((2, half_rows, cols_here), F32),
            pltpu.VMEM((2, half_rows, cols_here), F32),
            pltpu.VMEM((2, half_rows, cols_here), F32),
            pltpu.VMEM((2, Y_SIZE - 1, group_rows, cols_here), F32),
            pltpu.VMEM((2, Z_HIGH, group_rows, cols_here), F32),
            pltpu.VMEM((group_rows, cols_here), F32),
            pltpu.VMEM((scenarios, cols_here), F32),
            pltpu.VMEM((2, scenarios, rows_here), F32),
            pltpu.VMEM((2, chunk[1] // LANE, cols_size - 1, chunk[0], LANE), F32),
            pltpu.VMEM(chunk, F32),
            pltpu.VMEM((scenarios, rows_here), F32),
            pltpu.VMEM((3, group_rows, cols_here), F32),
            pltpu.VMEM((Z_HIGH, 3, scenarios), F32),
            pltpu.VMEM((cols_size, 5, scenarios), F32),
            pltpu.VMEM((plane, 5, scenarios), F32),
            pltpu.VMEM((cols_size, 1, scenarios), F32),
            pltpu.VMEM((plane, 1, scenarios), F32),
            pltpu.SemaphoreType.DMA((semaphores,)),
            pltpu.SemaphoreType.DMA((semaphores,)),
            pltpu.SemaphoreType.DMA((12 + rows_here // LANE,)),
        ],
        compiler_params=pltpu.CompilerParams(
            collective_id=0, has_side_effects=True, vmem_limit_bytes=32 << 20
        ),
    )(
        *[
            pltpu.with_memory_space_constraint(given, pltpu.HBM)
            for given in (
                values,
                tile_scale.T,
                occupancy.T,
                row_kind,
                right_side,
                cost_vector,
                lower_bound.reshape(1, -1),
                upper_bound.reshape(1, -1),
                x_start,
                y_start,
                step_sizes,
            )
        ]
    )
    results = (x_next, y_next, measures, move)
    x_next, y_next, measures, move = pl.pallas_call(
        write_out,
        out_shape=tuple(pltpu.HBM(r.shape, r.dtype) for r in results),
        in_specs=[vmem] * 4,
        out_specs=(hbm,) * 4,
        scratch_shapes=[pltpu.SemaphoreType.DMA((4,))],
    )(*[pltpu.with_memory_space_constraint(r, pltpu.VMEM) for r in results])
    return x_next, y_next, measures, move.reshape(-1)


def solution(mesh):
    return jax.shard_map(
        per_device,
        mesh=mesh,
        in_specs=(
            P("rows", "cols"),
            P("rows", "cols"),
            P("rows", "cols"),
            P("rows"),
            P(None, "rows"),
            P(None, "cols"),
            P("cols"),
            P("cols"),
            P(None, "cols"),
            P(None, "rows"),
            P(),
        ),
        out_specs=(P(None, "cols"), P(None, "rows"), P(), P()),
        check_vma=False,
    )
```

```python
import jax
import jax.numpy as jnp
from jax import lax
from jax.experimental import pallas as pl
from jax.experimental.pallas import tpu as pltpu
from jax.sharding import PartitionSpec as P

EPS = 1e-06
MESH = pl.DeviceIdType.MESH
F32 = jnp.float32
BF16 = jnp.bfloat16

Z_HIGH, Y_SIZE, CORES = 4, 8, 2
X_SIZE, Z_LOW = 4, 3
LANE = 128
TILE = 256


def ring_distance(offset, size):
    return min(offset, size - offset)


def kernel(
    values_in,
    scale_in,
    occupancy_in,
    kind_in,
    rhs_in,
    cost_in,
    low_in,
    high_in,
    x_in,
    y_in,
    step_in,
    x_out,
    y_out,
    measures_ref,
    move_ref,
    values,
    rhs,
    cost,
    x_start,
    y_start,
    scale_ref,
    occupancy_ref,
    kind_ref,
    low_ref,
    high_ref,
    step_ref,
    magnitude,
    col_peak,
    row_peak,
    col_first,
    row_first,
    col_second,
    col_scale,
    row_scale,
    scaled_duals,
    half_out,
    half_in,
    half,
    group_in,
    high_slots,
    dual_first,
    x_full,
    image,
    image_in,
    image_first,
    y_full,
    bounds_scaled,
    y_sums,
    early_cols,
    early_rows,
    late_cols,
    late_rows,
    send,
    recv,
    local,
):
    scenarios = x_full.shape[0]
    rows_here, cols_here = values.shape
    row_blocks, col_blocks = rows_here // LANE, cols_here // LANE
    per_tile = TILE // LANE
    group_rows = scenarios // (CORES * Y_SIZE)
    half_rows = scenarios // CORES
    chunk_rows = scenarios // X_SIZE
    chunk_cols = rows_here // Z_LOW
    rows_total = float(rows_here * Z_HIGH * Y_SIZE * CORES)
    cols_total = float(cols_here * X_SIZE * Z_LOW)

    rank, column = lax.axis_index("rows"), lax.axis_index("cols")
    core = lax.rem(rank, CORES)
    y = lax.rem(lax.div(rank, CORES), Y_SIZE)
    z_high = lax.div(rank, CORES * Y_SIZE)
    x = lax.div(column, Z_LOW)
    z_low = lax.rem(column, Z_LOW)
    group = core * Y_SIZE + y

    def at_rows(z_at, y_at, core_at):
        return ((z_at * Y_SIZE + y_at) * CORES + core_at, column)

    def at_cols(x_at, low_at):
        return (rank, x_at * Z_LOW + low_at)

    def shift(index, offset, size):
        return lax.rem(index + offset + size, size)

    y_offsets = sorted(range(1, Y_SIZE), key=lambda k: -ring_distance(k, Y_SIZE))
    plane_offsets = [
        (dy, dc) for dy in range(Y_SIZE) for dc in range(CORES) if (dy, dc) != (0, 0)
    ]
    plane_offsets.sort(key=lambda o: -ring_distance(o[0], Y_SIZE))
    z_offsets = sorted(range(1, Z_HIGH), key=lambda k: -ring_distance(k, Z_HIGH))
    col_offsets = [
        (dx, dl) for dx in range(X_SIZE) for dl in range(Z_LOW) if (dx, dl) != (0, 0)
    ]
    col_offsets.sort(key=lambda o: (o[1] == 0, -ring_distance(o[0], X_SIZE)))

    def plane_at(offset, sign):
        return shift(y, sign * offset[0], Y_SIZE), shift(core, sign * offset[1], CORES)

    def cols_at(offset, sign):
        return shift(x, sign * offset[0], X_SIZE), shift(z_low, sign * offset[1], Z_LOW)

    plane_to = [at_rows(z_high, *plane_at(o, 1)) for o in plane_offsets]
    z_to = [at_rows(shift(z_high, k, Z_HIGH), y, core) for k in z_offsets]
    y_to = [at_rows(z_high, shift(y, k, Y_SIZE), core) for k in y_offsets]
    cols_to = [at_cols(*cols_at(o, 1)) for o in col_offsets]
    partner = at_rows(z_high, y, 1 - core)

    started = []
    used = [0]

    def reserve(count):
        base = used[0]
        used[0] += count
        return base

    def copy(source, target, slot, device):
        return pltpu.make_async_remote_copy(
            src_ref=source,
            dst_ref=target,
            send_sem=send.at[slot],
            recv_sem=recv.at[slot],
            device_id=device,
            device_id_type=MESH,
        )

    def put(source, target, slot, device):
        moved = copy(source, target, slot, device)
        moved.start()
        started.append(moved)

    def arrived(target, slot, device):
        copy(target, target, slot, device).wait_recv()

    def spread(source, slots, peers):
        base = reserve(len(peers))
        for k, device in enumerate(peers):
            put(source, slots.at[k], base + k, device)
        return base

    def collect(slots, base, peers):
        for k, device in enumerate(peers):
            arrived(slots.at[k], base + k, device)

    def share(slots, own, targets):
        base = reserve(len(targets))
        for k, device in enumerate(targets):
            put(slots.at[own], slots.at[own], base + k, device)
        return base

    def added(slots, sources, base, targets):
        for k, device in enumerate(targets):
            arrived(slots.at[sources[k]], base + k, device)
        total = slots[0]
        for k in range(1, slots.shape[0]):
            total = total + slots[k]
        return total

    def block(index):
        return slice(index * LANE, (index + 1) * LANE)

    loads = [
        pltpu.make_async_copy(source, target, local.at[k])
        for k, (source, target) in enumerate(
            [
                (scale_in, scale_ref),
                (occupancy_in, occupancy_ref),
                (values_in, values),
                (y_in, y_start),
                (x_in, x_start),
                (cost_in, cost),
                (rhs_in, rhs),
                (low_in, low_ref),
                (high_in, high_ref),
                (step_in, step_ref),
            ]
            + [(kind_in.at[block(q)], kind_ref.at[q]) for q in range(row_blocks)]
        )
    ]
    for load in loads[:3]:
        load.start()
    barrier = pltpu.get_barrier_semaphore()
    everyone = plane_to + z_to + cols_to
    for device in everyone:
        pl.semaphore_signal(barrier, inc=1, device_id=device, device_id_type=MESH)
    loads[0].wait()
    loads[1].wait()

    factor = [
        [
            scale_ref[b, a] * occupancy_ref[b, a].astype(F32)
            for b in range(cols_here // TILE)
        ]
        for a in range(rows_here // TILE)
    ]

    def fold(array):
        return jnp.max(array.reshape(LANE // 8, 8, LANE), axis=0)

    loads[2].wait()
    for load in loads[3:]:
        load.start()
    col_best = [None] * col_blocks
    for q in range(row_blocks):
        across = None
        for l in range(col_blocks):
            entries = jnp.abs(values[block(q), block(l)].astype(F32)) * factor[q // per_tile][l // per_tile]
            magnitude[block(q), block(l)] = entries
            across = entries if across is None else jnp.maximum(across, entries)
            best = fold(entries)
            col_best[l] = best if q == 0 else jnp.maximum(col_best[l], best)
        row_peak[0, q : q + 1, :] = jnp.max(across.T, axis=0, keepdims=True)
    for l in range(col_blocks):
        col_peak[0, l : l + 1, :] = jnp.max(col_best[l], axis=0, keepdims=True)

    pl.semaphore_wait(barrier, len(everyone))
    plane_base = spread(col_peak.at[0], col_first.at[0], plane_to)
    row_base = spread(row_peak.at[0], row_first.at[0], cols_to)

    def best_of(own, slots, count):
        best = own
        for k in range(count):
            best = jnp.maximum(best, slots[k])
        return best

    collect(col_first.at[0], plane_base, plane_to)
    col_peak[1] = best_of(col_peak[0], col_first.at[0], len(plane_to))
    z_base = spread(col_peak.at[1], col_second.at[0], z_to)

    collect(row_first.at[0], row_base, cols_to)
    row_scale[0] = 1.0 / jnp.sqrt(best_of(row_peak[0], row_first.at[0], len(cols_to)) + EPS)

    for q in range(row_blocks):
        down = jnp.broadcast_to(row_scale[0, q : q + 1, :], (LANE, LANE)).T
        for l in range(col_blocks):
            best = fold(magnitude[block(q), block(l)] * down)
            col_best[l] = best if q == 0 else jnp.maximum(col_best[l], best)
    for l in range(col_blocks):
        col_peak[2, l : l + 1, :] = jnp.max(col_best[l], axis=0, keepdims=True)
    plane_base = spread(col_peak.at[2], col_first.at[1], plane_to)

    collect(col_second.at[0], z_base, z_to)
    col_scale[0] = 1.0 / jnp.sqrt(best_of(col_peak[1], col_second.at[0], len(z_to)) + EPS)

    for q in range(row_blocks):
        across = None
        for l in range(col_blocks):
            entries = magnitude[block(q), block(l)] * col_scale[0, l : l + 1, :]
            across = entries if across is None else jnp.maximum(across, entries)
        row_peak[1, q : q + 1, :] = jnp.max(across.T, axis=0, keepdims=True)
    row_base = spread(row_peak.at[1], row_first.at[1], cols_to)

    collect(col_first.at[1], plane_base, plane_to)
    col_peak[3] = best_of(col_peak[2], col_first.at[1], len(plane_to))
    z_base = spread(col_peak.at[3], col_second.at[1], z_to)

    loads[3].wait()
    collect(row_first.at[1], row_base, cols_to)
    peak = best_of(row_peak[1], row_first.at[1], len(cols_to))
    row_scale[1] = row_scale[0] / jnp.sqrt(row_scale[0] * peak + EPS)

    own_half = pl.ds(pl.multiple_of(core * half_rows, half_rows), half_rows)
    other_half = pl.ds(pl.multiple_of((1 - core) * half_rows, half_rows), half_rows)

    def group_of(core_at, y_at):
        start = (core_at * Y_SIZE + y_at) * group_rows
        return pl.ds(pl.multiple_of(start, group_rows), group_rows)

    def in_half(y_at):
        return pl.ds(pl.multiple_of(y_at * group_rows, group_rows), group_rows)

    def backward(duals, step):
        scaled = [
            jnp.concatenate(
                [
                    duals[:, block(q)] * row_scale[1, q : q + 1, :]
                    for q in range(a * per_tile, (a + 1) * per_tile)
                ],
                axis=1,
            ).astype(BF16)
            for a in range(rows_here // TILE)
        ]
        for a in range(rows_here // TILE):
            scaled_duals[:, a * TILE : (a + 1) * TILE] = scaled[a]

        def product(rows, target):
            for b in range(cols_here // TILE):
                at_b = slice(b * TILE, (b + 1) * TILE)
                total = None
                for a in range(rows_here // TILE):
                    at_a = slice(a * TILE, (a + 1) * TILE)
                    term = factor[a][b] * jnp.dot(
                        scaled_duals[rows, at_a], values[at_a, at_b], preferred_element_type=F32
                    )
                    total = term if total is None else total + term
                target[step, :, at_b] = total

        product(other_half, half_out)
        base = reserve(1)
        put(half_out.at[step], half_in.at[step], base, partner)
        product(own_half, half)
        return base

    def over_y(step, base):
        arrived(half_in.at[step], base, partner)
        half[step] = half[step] + half_in[step]
        base = reserve(len(y_offsets))
        for k, offset in enumerate(y_offsets):
            to = shift(y, offset, Y_SIZE)
            put(half.at[step, in_half(to), :], group_in.at[step, k], base + k, y_to[k])
        return base

    def over_z(step, base):
        for k, device in enumerate(y_to):
            arrived(group_in.at[step, k], base + k, device)
        total = half[step, in_half(y), :]
        for k in range(len(y_to)):
            total = total + group_in[step, k]
        high_slots[step, z_high] = total
        base = reserve(len(z_to))
        for k, device in enumerate(z_to):
            put(high_slots.at[step, z_high], high_slots.at[step, z_high], base + k, device)
        return base

    def z_slots_in(slots, base):
        for k, offset in enumerate(z_offsets):
            arrived(slots.at[shift(z_high, -offset, Z_HIGH)], base + k, z_to[k])
        total = slots[0]
        for k in range(1, Z_HIGH):
            total = total + slots[k]
        return total

    own_rows = pl.ds(pl.multiple_of(x * chunk_rows, chunk_rows), chunk_rows)
    pieces = chunk_cols // LANE

    def forward(vectors, step):
        scaled = [
            jnp.concatenate(
                [
                    vectors[:, block(l)] * col_scale[1, l : l + 1, :]
                    for l in range(b * per_tile, (b + 1) * per_tile)
                ],
                axis=1,
            ).astype(BF16)
            for b in range(cols_here // TILE)
        ]
        for a in range(rows_here // TILE):
            at_a = slice(a * TILE, (a + 1) * TILE)
            total = None
            for b in range(cols_here // TILE):
                term = factor[a][b] * lax.dot_general(
                    scaled[b],
                    values[at_a, b * TILE : (b + 1) * TILE],
                    (((1,), (1,)), ((), ())),
                    preferred_element_type=F32,
                )
                total = term if total is None else total + term
            image[step, :, at_a] = total

    def rows_of(x_at):
        return pl.ds(pl.multiple_of(x_at * chunk_rows, chunk_rows), chunk_rows)

    def lanes_of(low_at, piece):
        start = low_at * chunk_cols + piece * LANE
        return pl.ds(pl.multiple_of(start, LANE), LANE)

    def over_cols(step, piece):
        base = reserve(len(cols_to))
        for k, offset in enumerate(col_offsets):
            x_at, low_at = cols_at(offset, 1)
            source = image.at[step, rows_of(x_at), lanes_of(low_at, piece)]
            put(source, image_in.at[step, piece, k], base + k, cols_to[k])
        return base

    def image_sum(step, piece, base):
        for k, device in enumerate(cols_to):
            arrived(image_in.at[step, piece, k], base + k, device)
        total = image[step, own_rows, lanes_of(z_low, piece)]
        for k in range(len(cols_to)):
            total = total + image_in[step, piece, k]
        return total

    half_base = backward(y_start, 0)
    collect(col_second.at[1], z_base, z_to)
    peak = best_of(col_peak[3], col_second.at[1], len(z_to))
    col_scale[1] = col_scale[0] / jnp.sqrt(col_scale[0] * peak + EPS)
    group_base = over_y(0, half_base)
    loads[4].wait()
    forward(x_start, 0)
    z_base = over_z(0, group_base)
    for load in loads[5:]:
        load.wait()

    own_group = group_of(core, y)
    primal_step, dual_step = step_ref[0], step_ref[1]

    for l in range(col_blocks):
        col = col_scale[1, l : l + 1, :]
        wide = (group_rows, LANE)
        bounds_scaled[0, :, block(l)] = cost[own_group, block(l)] * col
        bounds_scaled[1, :, block(l)] = jnp.broadcast_to(low_ref[0:1, block(l)] / col, wide)
        bounds_scaled[2, :, block(l)] = jnp.broadcast_to(high_ref[0:1, block(l)] / col, wide)

    summed = z_slots_in(high_slots.at[0], z_base)
    for l in range(col_blocks):
        old = x_start[own_group, block(l)]
        cost_scaled, low_scaled, high_scaled = (bounds_scaled[k, :, block(l)] for k in range(3))
        dual = col_scale[1, l : l + 1, :] * summed[:, block(l)]
        dual_first[:, block(l)] = dual
        new = old - primal_step * (cost_scaled - dual)
        x_full[own_group, block(l)] = jnp.minimum(jnp.maximum(new, low_scaled), high_scaled)

    y_base = reserve(len(y_to))
    relay_base = reserve(Y_SIZE)
    for k, device in enumerate(y_to):
        put(x_full.at[own_group, :], x_full.at[own_group, :], y_base + k, device)
    put(x_full.at[own_group, :], x_full.at[own_group, :], relay_base + Y_SIZE - 1, partner)

    first_bases = [over_cols(0, piece) for piece in range(pieces)]

    for k in reversed(range(len(y_to))):
        rows = group_of(core, shift(y, -y_offsets[k], Y_SIZE))
        arrived(x_full.at[rows, :], y_base + k, y_to[k])
        put(x_full.at[rows, :], x_full.at[rows, :], relay_base + k, partner)
    for k, offset in enumerate(y_offsets + [0]):
        rows = group_of(1 - core, shift(y, -offset, Y_SIZE))
        arrived(x_full.at[rows, :], relay_base + k, partner)

    forward(x_full, 1)
    second_bases = [over_cols(1, piece) for piece in range(pieces)]
    for piece in range(pieces):
        image_first[:, block(piece)] = image_sum(0, piece, first_bases[piece])

    y_bases = []
    violations = products = moves = None

    def add(total, term):
        return term if total is None else total + term

    for piece in range(pieces):
        lanes = lanes_of(z_low, piece)
        line = pl.ds(z_low * pieces + piece, 1)
        scale = row_scale[1, line, :]
        y_old = y_start[own_rows, lanes]
        rhs_scaled = rhs[own_rows, lanes] * scale
        inequality = kind_ref[line, :] == 1
        first = scale * image_first[:, block(piece)]
        second = scale * image_sum(1, piece, second_bases[piece])
        trial = y_old + dual_step * (rhs_scaled - (2.0 * second - first))
        y_new = jnp.where(inequality, jnp.maximum(trial, 0.0), trial)
        y_full[own_rows, lanes] = y_new
        base = reserve(len(cols_to))
        for k, device in enumerate(cols_to):
            put(y_full.at[own_rows, lanes], y_full.at[own_rows, lanes], base + k, device)
        y_bases.append(base)
        violation = rhs_scaled - 0.5 * (first + second)
        violation = jnp.where(inequality, jnp.maximum(violation, 0.0), violation)
        violations = add(violations, violation * violation)
        products = add(products, rhs_scaled * (0.5 * (y_old + y_new)))
        moves = add(moves, (y_new - y_old) * (y_new - y_old))

    def on_lanes(terms, first_row):
        sums = jnp.sum(terms, axis=1, keepdims=True)
        shape = (terms.shape[0], scenarios)
        lanes = lax.broadcasted_iota(jnp.int32, shape, 1)
        rows = lax.broadcasted_iota(jnp.int32, shape, 0)
        spread_out = jnp.where(lanes == rows + first_row, jnp.broadcast_to(sums, shape), 0.0)
        return jnp.sum(spread_out, axis=0, keepdims=True)

    first_row = x * chunk_rows
    y_sums[z_high, 0:1, :] = on_lanes(violations, first_row)
    y_sums[z_high, 1:2, :] = on_lanes(products, first_row)
    y_sums[z_high, 2:3, :] = on_lanes(moves, first_row)
    sums_base = share(y_sums, z_high, z_to)

    for piece in range(pieces):
        for k, offset in enumerate(col_offsets):
            x_at, low_at = cols_at(offset, -1)
            target = y_full.at[rows_of(x_at), lanes_of(low_at, piece)]
            arrived(target, y_bases[piece] + k, cols_to[k])

    half_base = backward(y_full, 1)
    group_base = over_y(1, half_base)
    first_row = group * group_rows
    products = moves = None
    for l in range(col_blocks):
        old, new = x_start[own_group, block(l)], x_full[own_group, block(l)]
        products = add(products, bounds_scaled[0, :, block(l)] * (0.5 * (old + new)))
        moves = add(moves, (new - old) * (new - old))
    z_from = [shift(z_high, -k, Z_HIGH) for k in z_offsets]
    cols_from = [cols_at(o, -1)[0] * Z_LOW + cols_at(o, -1)[1] for o in col_offsets]
    plane_from = [plane_at(o, -1)[1] * Y_SIZE + plane_at(o, -1)[0] for o in plane_offsets]
    early_cols[column, 3:4, :] = on_lanes(products, first_row)
    early_cols[column, 4:5, :] = on_lanes(moves, first_row)
    early_cols[column, 0:3, :] = added(y_sums, z_from, sums_base, z_to)
    early_base = share(early_cols, column, cols_to)
    z_base = over_z(1, group_base)
    x_written = pltpu.make_async_copy(x_full, x_out, local.at[len(loads)])
    x_written.start()
    y_written = pltpu.make_async_copy(y_full, y_out, local.at[len(loads) + 1])
    y_written.start()
    early_rows[group] = added(early_cols, cols_from, early_base, cols_to)
    early_base = share(early_rows, group, plane_to)
    summed = z_slots_in(high_slots.at[1], z_base)
    bounds = None
    for l in range(col_blocks):
        cost_scaled, low_scaled, high_scaled = (bounds_scaled[k, :, block(l)] for k in range(3))
        dual = col_scale[1, l : l + 1, :] * summed[:, block(l)]
        reduced = cost_scaled - 0.5 * (dual_first[:, block(l)] + dual)
        bound = low_scaled * jnp.maximum(reduced, 0.0) - high_scaled * jnp.maximum(-reduced, 0.0)
        bounds = bound if bounds is None else bounds + bound
    late_cols[column] = on_lanes(bounds, first_row)
    base = share(late_cols, column, cols_to)
    late_rows[group] = added(late_cols, cols_from, base, cols_to)
    base = share(late_rows, group, plane_to)
    total = added(early_rows, plane_from, early_base, plane_to)
    measures_ref[0:1, :] = total[0:1, :] / rows_total
    measures_ref[2:3, :] = total[2:3, :] / rows_total
    move_ref[...] = total[4:5, :] / cols_total
    x_written.wait()
    y_written.wait()
    for moved in started[: -len(plane_to)]:
        moved.wait_send()
    bound_total = added(late_rows, plane_from, base, plane_to)
    measures_ref[1:2, :] = (total[3:4, :] - total[1:2, :] - bound_total) / cols_total
    for moved in started[-len(plane_to) :]:
        moved.wait_send()


def write_out(*refs):
    sources, targets, done = refs[:4], refs[4:8], refs[8]
    writes = [pltpu.make_async_copy(sources[k], targets[k], done.at[k]) for k in range(4)]
    for write in writes:
        write.start()
    for write in writes:
        write.wait()


def per_device(
    values,
    tile_scale,
    occupancy,
    row_kind,
    right_side,
    cost_vector,
    lower_bound,
    upper_bound,
    x_start,
    y_start,
    step_sizes,
):
    rows_here, cols_here = values.shape
    scenarios = x_start.shape[0]
    plane, cols_size = CORES * Y_SIZE, X_SIZE * Z_LOW
    row_blocks, col_blocks = rows_here // LANE, cols_here // LANE
    group_rows, half_rows = scenarios // plane, scenarios // CORES
    chunk = (scenarios // X_SIZE, rows_here // Z_LOW)
    semaphores = 2 * (plane + Z_HIGH + cols_size - 3) + 2 * (1 + Y_SIZE + Z_HIGH - 2)
    semaphores += 2 * Y_SIZE - 1 + 3 * (chunk[1] // LANE) * (cols_size - 1) + Z_HIGH - 1 + 2 * (cols_size - 1 + plane - 1)
    vmem, hbm, anywhere = (
        pl.BlockSpec(memory_space=space) for space in (pltpu.VMEM, pltpu.HBM, pl.ANY)
    )
    x_next, y_next, measures, move = pl.pallas_call(
        kernel,
        out_shape=(
            pltpu.VMEM((scenarios, cols_here), F32),
            pltpu.VMEM((scenarios, rows_here), F32),
            pltpu.VMEM((3, scenarios), F32),
            pltpu.VMEM((1, scenarios), F32),
        ),
        in_specs=[hbm] * 11,
        out_specs=(anywhere, anywhere, vmem, vmem),
        scratch_shapes=[
            pltpu.VMEM((rows_here, cols_here), BF16),
            pltpu.VMEM((scenarios, rows_here), F32),
            pltpu.VMEM((scenarios, cols_here), F32),
            pltpu.VMEM((scenarios, cols_here), F32),
            pltpu.VMEM((scenarios, rows_here), F32),
            pltpu.SMEM((cols_here // TILE, rows_here // TILE), F32),
            pltpu.SMEM((cols_here // TILE, rows_here // TILE), jnp.int32),
            pltpu.VMEM((8, LANE), jnp.int32),
            pltpu.VMEM((1, cols_here), F32),
            pltpu.VMEM((1, cols_here), F32),
            pltpu.SMEM((2,), F32),
            pltpu.VMEM((rows_here, cols_here), F32),
            pltpu.VMEM((4, col_blocks, LANE), F32),
            pltpu.VMEM((2, row_blocks, LANE), F32),
            pltpu.VMEM((2, plane - 1, col_blocks, LANE), F32),
            pltpu.VMEM((2, cols_size - 1, row_blocks, LANE), F32),
            pltpu.VMEM((2, Z_HIGH - 1, col_blocks, LANE), F32),
            pltpu.VMEM((2, col_blocks, LANE), F32),
            pltpu.VMEM((2, row_blocks, LANE), F32),
            pltpu.VMEM((scenarios, rows_here), BF16),
            pltpu.VMEM((2, half_rows, cols_here), F32),
            pltpu.VMEM((2, half_rows, cols_here), F32),
            pltpu.VMEM((2, half_rows, cols_here), F32),
            pltpu.VMEM((2, Y_SIZE - 1, group_rows, cols_here), F32),
            pltpu.VMEM((2, Z_HIGH, group_rows, cols_here), F32),
            pltpu.VMEM((group_rows, cols_here), F32),
            pltpu.VMEM((scenarios, cols_here), F32),
            pltpu.VMEM((2, scenarios, rows_here), F32),
            pltpu.VMEM((2, chunk[1] // LANE, cols_size - 1, chunk[0], LANE), F32),
            pltpu.VMEM(chunk, F32),
            pltpu.VMEM((scenarios, rows_here), F32),
            pltpu.VMEM((3, group_rows, cols_here), F32),
            pltpu.VMEM((Z_HIGH, 3, scenarios), F32),
            pltpu.VMEM((cols_size, 5, scenarios), F32),
            pltpu.VMEM((plane, 5, scenarios), F32),
            pltpu.VMEM((cols_size, 1, scenarios), F32),
            pltpu.VMEM((plane, 1, scenarios), F32),
            pltpu.SemaphoreType.DMA((semaphores,)),
            pltpu.SemaphoreType.DMA((semaphores,)),
            pltpu.SemaphoreType.DMA((12 + rows_here // LANE,)),
        ],
        compiler_params=pltpu.CompilerParams(
            collective_id=0, has_side_effects=True, vmem_limit_bytes=32 << 20
        ),
    )(
        *[
            pltpu.with_memory_space_constraint(given, pltpu.HBM)
            for given in (
                values,
                tile_scale.T,
                occupancy.T,
                row_kind,
                right_side,
                cost_vector,
                lower_bound.reshape(1, -1),
                upper_bound.reshape(1, -1),
                x_start,
                y_start,
                step_sizes,
            )
        ]
    )
    results = (x_next, y_next, measures, move)
    x_next, y_next, measures, move = pl.pallas_call(
        write_out,
        out_shape=tuple(pltpu.HBM(r.shape, r.dtype) for r in results),
        in_specs=[vmem] * 4,
        out_specs=(hbm,) * 4,
        scratch_shapes=[pltpu.SemaphoreType.DMA((4,))],
    )(*[pltpu.with_memory_space_constraint(r, pltpu.VMEM) for r in results])
    return x_next, y_next, measures, move.reshape(-1)


def solution(mesh):
    return jax.shard_map(
        per_device,
        mesh=mesh,
        in_specs=(
            P("rows", "cols"),
            P("rows", "cols"),
            P("rows", "cols"),
            P("rows"),
            P(None, "rows"),
            P(None, "cols"),
            P("cols"),
            P("cols"),
            P(None, "cols"),
            P(None, "rows"),
            P(),
        ),
        out_specs=(P(None, "cols"), P(None, "rows"), P(), P()),
        check_vma=False,
    )
```
